32 devices in a mesh: groups: 2 (over x), wide: 16 (over z, y, core).
Axes of the slice: x: 2, y: 2, z: 4, core: 2. Of those that a mesh axis runs over, the one named last changes fastest.
Arguments:
- video: bfloat16 [64, 1024, 1152], P(('groups', 'wide')), parts along dimension 0, may hold values from -40 to 40
- modulation: float32 [12, 1152], P('groups'), parts along dimension 0, may hold values from -3 to 3
- spatial_input: bfloat16 [1152, 3456], replicated, may hold values from -1 to 1
- spatial_output: bfloat16 [1152, 1152], replicated, may hold values from -0.1875 to 0.1875
- temporal_input: bfloat16 [1152, 3456], replicated, may hold values from -1 to 1
- temporal_output: bfloat16 [1152, 1152], replicated, may hold values from -0.1875 to 0.1875
Outputs:
- refined: bfloat16 [64, 1024, 1152], P(('groups', 'wide')), parts along dimension 0
The draws below stay inside these ranges and needn't reach their ends.
There are 2 independent parts, one for each index of `groups`. The reference program is written for one: setup_inputs(seed, part) draws one part's arguments, and reference() takes and returns one part's arrays. A program takes and returns all parts, laid end to end along the dimension named above; an argument that names none is the same for every part. Nothing has to cross between parts.
All inputs are finite; a program needn't handle non-finite values.
Results may differ from the reference program's by a relative error of at most 0.0052.
Values may be sent and summed in bfloat16 or wider, within the bound.
No kernel may reach another device: no remote copies, remote signals or barrier semaphores. Data moves between devices by JAX's collectives and lax.ppermute only.
A program may use at most 320 MiB of HBM per device.

```python
import math
import jax
import jax.numpy as jnp
from jax import lax

D = 1152
HEADS = 16
HEAD_DIM = 72
F = 32
S = 1024


def drawn_weight(key, marker):
    drawn = jax.random.normal(jax.random.fold_in(key, marker), (D, 3 * D), jnp.float32)
    drawn = jnp.clip(drawn, -5.0, 5.0) / math.sqrt(D)
    drawn = jnp.clip(drawn, -1.0, 1.0)
    return drawn.astype(jnp.bfloat16)


def draw_spatial_input(key, part):
    return drawn_weight(key, 11)


def draw_temporal_input(key, part):
    return drawn_weight(key, 23)


def draw_video(key, part):
    streams = jax.random.split(key, 3)
    baseline = jax.random.normal(streams[0], (F, S, D), jnp.float32)
    column = jnp.exp(jax.random.uniform(streams[1], (D,), jnp.float32, math.log(0.3), math.log(3.0)))
    rowwise = jnp.exp(jax.random.uniform(streams[2], (F, S, 1), jnp.float32, math.log(0.3), math.log(3.0)))
    video = baseline * column * rowwise
    return jnp.clip(video, -40.0, 40.0).astype(jnp.bfloat16)


def normal_values(stream_key, extent, scale, most, dtype=jnp.bfloat16):
    values = jax.random.normal(stream_key, extent, jnp.float32) * scale
    return jnp.minimum(jnp.maximum(values, -most), most).astype(dtype)


def setup_inputs(seed: int = 0, part: int = 0) -> dict:
    keys = jax.random.split(jax.random.key(seed), 7)
    own_keys = jax.random.split(jax.random.fold_in(keys[6], part), 7)
    video = draw_video(jax.random.fold_in(jax.random.fold_in(keys[6], part), 71), part)
    modulation = normal_values(own_keys[1], (6, D), 0.5, 3.0, jnp.float32)
    spatial_input = draw_spatial_input(jax.random.fold_in(keys[6], 71), part)
    spatial_output = normal_values(keys[3], (D, D), D ** -0.5, 0.1875)
    temporal_input = draw_temporal_input(jax.random.fold_in(keys[6], 71), part)
    temporal_output = normal_values(keys[5], (D, D), D ** -0.5, 0.1875)
    return dict(video=video, modulation=modulation, spatial_input=spatial_input, spatial_output=spatial_output, temporal_input=temporal_input, temporal_output=temporal_output)


epsilon = 1e-06

def normalize(stream, offset_row, stretch):
    values = stream.astype(jnp.float32)
    average = lax.optimization_barrier(jnp.mean(values, axis=-1, keepdims=True))
    centered = values - average
    spread = lax.optimization_barrier(jnp.mean(centered * centered, axis=-1, keepdims=True))
    return (centered * lax.rsqrt(spread + epsilon) * (1.0 + stretch) + offset_row).astype(jnp.bfloat16)

def space_frame(frame, modulation, spatial_input, spatial_output):
    score_scale = 1.0 / math.sqrt(HEAD_DIM)
    normed = normalize(frame, modulation[0], modulation[1])
    triples = jnp.dot(normed, spatial_input, preferred_element_type=jnp.float32).astype(jnp.bfloat16)
    triples = triples.reshape(S, 3, HEADS, HEAD_DIM).astype(jnp.float32)
    scores = jnp.einsum('qhd,khd->hqk', triples[:, 0], triples[:, 1]) * score_scale
    weights = jax.nn.softmax(scores, axis=-1).astype(jnp.bfloat16)
    attended = jnp.einsum('hqk,khd->qhd', weights.astype(jnp.float32), triples[:, 2]).astype(jnp.bfloat16)
    branch = jnp.dot(attended.reshape(S, D), spatial_output, preferred_element_type=jnp.float32)
    return (frame.astype(jnp.float32) + modulation[2] * branch).astype(jnp.bfloat16)

def reference(video, modulation, spatial_input, spatial_output, temporal_input, temporal_output):
    score_scale = 1.0 / math.sqrt(HEAD_DIM)
    halfway = lax.map(lambda frame: space_frame(frame, modulation, spatial_input, spatial_output), video)
    normed = normalize(halfway, modulation[3], modulation[4])
    triples = jnp.dot(normed.reshape(F * S, D), temporal_input, preferred_element_type=jnp.float32).astype(jnp.bfloat16)
    triples = triples.reshape(F, S, 3, HEADS, HEAD_DIM).astype(jnp.float32)
    scores = jnp.einsum('fshd,gshd->shfg', triples[:, :, 0], triples[:, :, 1]) * score_scale
    weights = jax.nn.softmax(scores, axis=-1).astype(jnp.bfloat16)
    attended = jnp.einsum('shfg,gshd->fshd', weights.astype(jnp.float32), triples[:, :, 2]).astype(jnp.bfloat16)
    branch = jnp.dot(attended.reshape(F * S, D), temporal_output, preferred_element_type=jnp.float32)
    return (halfway.astype(jnp.float32) + modulation[5] * branch.reshape(F, S, D)).astype(jnp.bfloat16)
```

```python
import functools
import math

import jax
import jax.numpy as jnp
from jax import lax
from jax.experimental import pallas as pl
from jax.experimental.pallas import tpu as pltpu
from jax.sharding import PartitionSpec as P

HEADS = 16
HEAD_DIM = 72
EPSILON = 1e-06
SCORE_SCALE = math.log2(math.e) / math.sqrt(HEAD_DIM)
LANES = 128
WINDOW = 2 * LANES
FAR = -1e30
VMEM_LIMIT = 56 * 1024 * 1024
FORWARD = (1, 1, 2)
BACKWARD = ((0, 1), (2,))


def normalize(values, offset_row, stretch):
    average = jnp.mean(values, axis=-1, keepdims=True)
    centered = values - average
    spread = jnp.mean(centered * centered, axis=-1, keepdims=True)
    return (centered * lax.rsqrt(spread + EPSILON) * (1.0 + stretch) + offset_row).astype(
        jnp.bfloat16
    )


def head_window(head, features):
    tile = min(head * HEAD_DIM // LANES, features // LANES - 2)
    return tile * LANES, head * HEAD_DIM - tile * LANES


def in_head(rows, first):
    lane = lax.broadcasted_iota(jnp.int32, (rows, WINDOW), 1)
    return (lane >= first) & (lane < first + HEAD_DIM)


def attend(q_of, k_of, v_of, rows, keys, features, total, total_row, allowed=None):
    for head in range(HEADS):
        lane, first = head_window(head, features)
        mine = in_head(keys, first)
        key = jnp.where(mine, k_of(lane), 0)
        value = jnp.where(mine, v_of(lane), 0)
        scores = lax.dot_general(
            q_of(lane), key, (((1,), (1,)), ((), ())), preferred_element_type=jnp.float32
        )
        if allowed is not None:
            scores = jnp.where(allowed, scores, FAR)
        largest = jnp.max(scores, axis=-1, keepdims=True)
        powers = jnp.exp2(scores - largest)
        weight = jnp.sum(powers, axis=-1, keepdims=True)
        mixed = jnp.dot(powers.astype(jnp.bfloat16), value, preferred_element_type=jnp.float32)
        mixed = mixed * (1.0 / weight)
        here = (pl.ds(total_row, rows), pl.ds(lane, WINDOW))
        if head == 0:
            total[pl.ds(total_row, rows), :] = jnp.zeros((rows, features), jnp.float32)
        total[here] = total[here] + mixed


def project_space_kernel(x_ref, mod_ref, w_ref, o_ref, normed):
    part = pl.program_id(0)
    block = pl.program_id(1)
    rows = x_ref.shape[0]
    here = pl.ds(pl.multiple_of(block * rows, rows), rows)

    @pl.when(part == 0)
    def _():
        normed[here, :] = normalize(
            x_ref[...].astype(jnp.float32), mod_ref[0:1, :], mod_ref[1:2, :]
        )

    product = jnp.dot(normed[here, :], w_ref[...], preferred_element_type=jnp.float32)
    o_ref[...] = (product * jnp.where(part == 0, SCORE_SCALE, 1.0)).astype(jnp.bfloat16)


def project_space(video, modulation, weights):
    frames, sites, features = video.shape
    rows = frames * sites
    block = min(512, rows)
    return pl.pallas_call(
        project_space_kernel,
        out_shape=jax.ShapeDtypeStruct((rows, 3 * features), jnp.bfloat16),
        grid=(3, rows // block),
        in_specs=[
            pl.BlockSpec((block, features), lambda n, r: (jnp.where(n == 0, r, 0), 0)),
            pl.BlockSpec(modulation.shape, lambda n, r: (0, 0)),
            pl.BlockSpec((features, features), lambda n, r: (0, n)),
        ],
        out_specs=pl.BlockSpec((block, features), lambda n, r: (r, n)),
        scratch_shapes=[pltpu.VMEM((rows, features), jnp.bfloat16)],
        compiler_params=pltpu.CompilerParams(vmem_limit_bytes=VMEM_LIMIT),
        cost_estimate=pl.CostEstimate(
            flops=2 * rows * features * 3 * features,
            bytes_accessed=2 * (4 * rows * features + 3 * features * features),
            transcendentals=0,
        ),
        name="space_project",
    )(video.reshape(rows, features), modulation, weights)


def attend_space_kernel(x_ref, q_ref, k_ref, v_ref, mod_ref, w_ref, o_ref, total):
    rows, features = q_ref.shape
    keys = k_ref.shape[0]
    attend(
        lambda lane: q_ref[:, pl.ds(lane, WINDOW)],
        lambda lane: k_ref[:, pl.ds(lane, WINDOW)],
        lambda lane: v_ref[:, pl.ds(lane, WINDOW)],
        rows,
        keys,
        features,
        total,
        0,
    )
    branch = jnp.dot(
        total[...].astype(jnp.bfloat16), w_ref[...], preferred_element_type=jnp.float32
    )
    halfway = x_ref[0].astype(jnp.float32) + mod_ref[2:3, :] * branch
    o_ref[...] = halfway.astype(jnp.bfloat16).reshape(o_ref.shape)


def attend_space(video, triples, modulation, weights, first, count, devices):
    frames, sites, features = video.shape
    block = 256
    per = count // devices
    blocks = sites // block
    start = first // block
    return pl.pallas_call(
        attend_space_kernel,
        out_shape=jax.ShapeDtypeStruct((devices, frames, per, features), jnp.bfloat16),
        grid=(frames, count // block),
        in_specs=[
            pl.BlockSpec((1, block, features), lambda f, q: (f, start + q, 0)),
            pl.BlockSpec((block, features), lambda f, q: (f * blocks + start + q, 0)),
            pl.BlockSpec((sites, features), lambda f, q: (f, 1)),
            pl.BlockSpec((sites, features), lambda f, q: (f, 2)),
            pl.BlockSpec(modulation.shape, lambda f, q: (0, 0)),
            pl.BlockSpec(weights.shape, lambda f, q: (0, 0)),
        ],
        out_specs=pl.BlockSpec((block // per, 1, per, features), lambda f, q: (q, f, 0, 0)),
        scratch_shapes=[pltpu.VMEM((block, features), jnp.float32)],
        compiler_params=pltpu.CompilerParams(vmem_limit_bytes=VMEM_LIMIT),
        cost_estimate=pl.CostEstimate(
            flops=2 * frames * count * (features * features + 2 * sites * HEADS * WINDOW),
            bytes_accessed=2 * features * (frames * (3 * count + 2 * sites) + features),
            transcendentals=frames * count * sites * HEADS,
        ),
        name="space_attend",
    )(video, triples, triples, triples, modulation, weights)


def time_kernel(x_ref, mod_ref, wi_ref, wo_ref, o_ref, triples, total):
    devices, frames, per, features = x_ref.shape
    steps = devices * frames
    groups = per // 8
    size = steps * 8
    values = x_ref[...].astype(jnp.float32).reshape(steps, per, features)
    values = jnp.concatenate(
        [values[:, 8 * g : 8 * g + 8, :].reshape(size, features) for g in range(groups)], axis=0
    )
    normed = normalize(values, mod_ref[3:4, :], mod_ref[4:5, :])
    for part in range(3):
        lanes = pl.ds(part * features, features)
        product = jnp.dot(normed, wi_ref[:, lanes], preferred_element_type=jnp.float32)
        if part == 0:
            product = product * SCORE_SCALE
        triples[:, lanes] = product.astype(jnp.bfloat16)
    site_of_query = lax.broadcasted_iota(jnp.int32, (size, size), 0) % 8
    site_of_key = lax.broadcasted_iota(jnp.int32, (size, size), 1) % 8
    allowed = site_of_query == site_of_key
    for g in range(groups):
        here = pl.ds(g * size, size)
        attend(
            lambda lane: triples[here, pl.ds(lane, WINDOW)],
            lambda lane: triples[here, pl.ds(features + lane, WINDOW)],
            lambda lane: triples[here, pl.ds(2 * features + lane, WINDOW)],
            size,
            size,
            features,
            total,
            g * size,
            allowed,
        )
    branch = jnp.dot(
        total[...].astype(jnp.bfloat16), wo_ref[...], preferred_element_type=jnp.float32
    )
    refined = values + mod_ref[5:6, :] * branch
    refined = jnp.concatenate(
        [
            refined[g * size : (g + 1) * size].reshape(steps, 8, features)
            for g in range(groups)
        ],
        axis=1,
    )
    o_ref[...] = refined.astype(jnp.bfloat16).reshape(o_ref.shape)


def attend_time(halfway, modulation, wide_weights, weights):
    devices, frames, per, features = halfway.shape
    block = min(16, per)
    rows = devices * frames * block
    spec = pl.BlockSpec((devices, frames, block, features), lambda s: (0, 0, s, 0))
    return pl.pallas_call(
        time_kernel,
        out_shape=jax.ShapeDtypeStruct(halfway.shape, jnp.bfloat16),
        grid=(per // block,),
        in_specs=[
            spec,
            pl.BlockSpec(modulation.shape, lambda s: (0, 0)),
            pl.BlockSpec(wide_weights.shape, lambda s: (0, 0), pipeline_mode=pl.Buffered(1)),
            pl.BlockSpec(weights.shape, lambda s: (0, 0), pipeline_mode=pl.Buffered(1)),
        ],
        out_specs=spec,
        scratch_shapes=[
            pltpu.VMEM((rows, 3 * features), jnp.bfloat16),
            pltpu.VMEM((rows, features), jnp.float32),
        ],
        compiler_params=pltpu.CompilerParams(vmem_limit_bytes=VMEM_LIMIT),
        cost_estimate=pl.CostEstimate(
            flops=2 * halfway.size * (4 * features + 2 * 8 * devices * frames * HEADS * WINDOW // features),
            bytes_accessed=4 * halfway.size + 8 * features * features,
            transcendentals=halfway.size // features * 8 * devices * frames * HEADS,
        ),
        name="time_block",
    )(halfway, modulation, wide_weights, weights)


def exchange(pieces):
    return lax.all_to_all(pieces, "wide", split_axis=0, concat_axis=0, tiled=True)


def on_device(video, modulation, spatial_input, spatial_output, temporal_input, temporal_output):
    frames, sites, features = video.shape
    devices = lax.axis_size("wide")
    triples = project_space(video, modulation, spatial_input)
    unit = sites // sum(FORWARD)
    first = 0
    arrived = []
    for share in FORWARD:
        count = share * unit
        halfway = attend_space(
            video, triples, modulation, spatial_output, first, count, devices
        )
        arrived.append(exchange(halfway))
        first += count
    refined = []
    for members in BACKWARD:
        done = [
            attend_time(arrived[m], modulation, temporal_input, temporal_output) for m in members
        ]
        back = exchange(done[0] if len(done) == 1 else jnp.concatenate(done, axis=2))
        place = 0
        for m in members:
            per = arrived[m].shape[2]
            piece = back[:, :, place : place + per]
            refined.append(piece.transpose(1, 0, 2, 3).reshape(frames, devices * per, features))
            place += per
    return jnp.concatenate(refined, axis=1)


def solution(mesh):
    placed = (P(("groups", "wide"), None, None), P("groups", None), P(), P(), P(), P())
    return jax.shard_map(
        on_device,
        mesh=mesh,
        in_specs=placed,
        out_specs=P(("groups", "wide"), None, None),
        check_vma=False,
    )
```

```python
import functools
import math

import jax
import jax.numpy as jnp
from jax import lax
from jax.experimental import pallas as pl
from jax.experimental.pallas import tpu as pltpu
from jax.sharding import PartitionSpec as P

HEADS = 16
HEAD_DIM = 72
EPSILON = 1e-06
SCORE_SCALE = math.log2(math.e) / math.sqrt(HEAD_DIM)
LANES = 128
WINDOW = 2 * LANES
FAR = -1e30
VMEM_LIMIT = 63 * 1024 * 1024
FORWARD = (1, 1, 2)
BACKWARD = ((0, 1), (2,))


def normalize(values, offset_row, stretch):
    average = jnp.mean(values, axis=-1, keepdims=True)
    centered = values - average
    spread = jnp.mean(centered * centered, axis=-1, keepdims=True)
    return (centered * lax.rsqrt(spread + EPSILON) * (1.0 + stretch) + offset_row).astype(
        jnp.bfloat16
    )


def head_window(head, features):
    last = features // LANES - 2
    if isinstance(head, int):
        tile = min(head * HEAD_DIM // LANES, last)
        return tile * LANES, head * HEAD_DIM - tile * LANES
    tile = jnp.minimum(head * HEAD_DIM // LANES, last)
    return pl.multiple_of(tile * LANES, LANES), head * HEAD_DIM - tile * LANES


def attend_head(head, q_of, k_of, v_of, total, rows, features, allowed=None):
    lane, first = head_window(head, features)
    lanes = lax.broadcasted_iota(jnp.int32, (rows.size, WINDOW), 1)
    mine = (lanes >= first) & (lanes < first + HEAD_DIM)
    scores = lax.dot_general(
        jnp.where(mine, q_of(lane), 0),
        k_of(lane),
        (((1,), (1,)), ((), ())),
        preferred_element_type=jnp.float32,
    )
    if allowed is not None:
        scores = jnp.where(allowed, scores, FAR)
    largest = jnp.max(scores, axis=-1, keepdims=True)
    powers = jnp.exp2(scores - largest)
    weight = jnp.sum(powers, axis=-1, keepdims=True)
    mixed = jnp.dot(powers.astype(jnp.bfloat16), v_of(lane), preferred_element_type=jnp.float32)
    mixed = jnp.where(mine, mixed * (1.0 / weight), 0.0)
    total[rows, pl.ds(lane, WINDOW)] = total[rows, pl.ds(lane, WINDOW)] + mixed


def project_space_kernel(x_ref, mod_ref, w_ref, o_ref):
    features = x_ref.shape[1]
    normed = normalize(x_ref[...].astype(jnp.float32), mod_ref[0:1, :], mod_ref[1:2, :])
    product = jnp.dot(normed, w_ref[...], preferred_element_type=jnp.float32)
    o_ref[:, :features] = (product[:, :features] * SCORE_SCALE).astype(jnp.bfloat16)
    o_ref[:, features:] = product[:, features:].astype(jnp.bfloat16)


def project_space(video, modulation, weights):
    frames, sites, features = video.shape
    rows = frames * sites
    block = 256
    return pl.pallas_call(
        project_space_kernel,
        out_shape=jax.ShapeDtypeStruct((rows, 3 * features), jnp.bfloat16),
        grid=(rows // block,),
        in_specs=[
            pl.BlockSpec((block, features), lambda r: (r, 0)),
            pl.BlockSpec(modulation.shape, lambda r: (0, 0)),
            pl.BlockSpec(weights.shape, lambda r: (0, 0), pipeline_mode=pl.Buffered(1)),
        ],
        out_specs=pl.BlockSpec((block, 3 * features), lambda r: (r, 0)),
        compiler_params=pltpu.CompilerParams(vmem_limit_bytes=VMEM_LIMIT),
        cost_estimate=pl.CostEstimate(
            flops=2 * rows * features * 3 * features,
            bytes_accessed=2 * (4 * rows * features + 3 * features * features),
            transcendentals=0,
        ),
        name="space_project",
    )(video.reshape(rows, features), modulation, weights)


def attend_space_kernel(x_ref, q_ref, k_ref, v_ref, mod_ref, w_ref, o_ref, total):
    rows, features = q_ref.shape
    total[...] = jnp.zeros_like(total)
    for head in range(HEADS):
        attend_head(
            head,
            lambda lane: q_ref[:, pl.ds(lane, WINDOW)],
            lambda lane: k_ref[:, pl.ds(lane, WINDOW)],
            lambda lane: v_ref[:, pl.ds(lane, WINDOW)],
            total,
            pl.ds(0, rows),
            features,
        )
    branch = jnp.dot(
        total[...].astype(jnp.bfloat16), w_ref[...], preferred_element_type=jnp.float32
    )
    halfway = x_ref[0].astype(jnp.float32) + mod_ref[2:3, :] * branch
    o_ref[...] = halfway.astype(jnp.bfloat16).reshape(o_ref.shape)


def attend_space(video, triples, modulation, weights, first, count, devices):
    frames, sites, features = video.shape
    block = 256
    per = count // devices
    blocks = sites // block
    start = first // block
    return pl.pallas_call(
        attend_space_kernel,
        out_shape=jax.ShapeDtypeStruct((devices, frames, per, features), jnp.bfloat16),
        grid=(frames, count // block),
        in_specs=[
            pl.BlockSpec((1, block, features), lambda f, q: (f, start + q, 0)),
            pl.BlockSpec((block, features), lambda f, q: (f * blocks + start + q, 0)),
            pl.BlockSpec((sites, features), lambda f, q: (f, 1)),
            pl.BlockSpec((sites, features), lambda f, q: (f, 2)),
            pl.BlockSpec(modulation.shape, lambda f, q: (0, 0)),
            pl.BlockSpec(weights.shape, lambda f, q: (0, 0)),
        ],
        out_specs=pl.BlockSpec((block // per, 1, per, features), lambda f, q: (q, f, 0, 0)),
        scratch_shapes=[pltpu.VMEM((block, features), jnp.float32)],
        compiler_params=pltpu.CompilerParams(vmem_limit_bytes=VMEM_LIMIT),
        cost_estimate=pl.CostEstimate(
            flops=2 * frames * count * (features * features + 2 * sites * HEADS * WINDOW),
            bytes_accessed=2 * features * (frames * (3 * count + 2 * sites) + features),
            transcendentals=frames * count * sites * HEADS,
        ),
        name="space_attend",
    )(video, triples, triples, triples, modulation, weights)


def time_kernel(x_ref, mod_ref, wi_ref, wo_ref, *rest):
    o_ref, triples, total = rest[-3:]
    devices, frames, per, features = x_ref.shape
    steps = devices * frames
    groups = per // 8
    size = steps * 8
    values = x_ref[...].astype(jnp.float32).reshape(steps, per, features)
    values = jnp.concatenate(
        [values[:, 8 * g : 8 * g + 8, :].reshape(size, features) for g in range(groups)], axis=0
    )
    normed = normalize(values, mod_ref[3:4, :], mod_ref[4:5, :])
    for part in range(3):
        lanes = pl.ds(part * features, features)
        product = jnp.dot(normed, wi_ref[:, lanes], preferred_element_type=jnp.float32)
        if part == 0:
            product = product * SCORE_SCALE
        triples[:, lanes] = product.astype(jnp.bfloat16)
    total[...] = jnp.zeros_like(total)
    site_of_query = lax.broadcasted_iota(jnp.int32, (size, size), 0) % 8
    site_of_key = lax.broadcasted_iota(jnp.int32, (size, size), 1) % 8

    def body(head, carry):
        for g in range(groups):
            here = pl.ds(g * size, size)
            attend_head(
                head,
                lambda lane: triples[here, pl.ds(lane, WINDOW)],
                lambda lane: triples[here, pl.ds(pl.multiple_of(features + lane, LANES), WINDOW)],
                lambda lane: triples[
                    here, pl.ds(pl.multiple_of(2 * features + lane, LANES), WINDOW)
                ],
                total,
                here,
                features,
                site_of_query == site_of_key,
            )
        return carry

    lax.fori_loop(0, HEADS, body, 0, unroll=4)
    branch = jnp.dot(
        total[...].astype(jnp.bfloat16), wo_ref[...], preferred_element_type=jnp.float32
    )
    refined = values + mod_ref[5:6, :] * branch
    refined = jnp.concatenate(
        [
            refined[g * size : (g + 1) * size].reshape(steps, 8, features)
            for g in range(groups)
        ],
        axis=1,
    )
    o_ref[...] = refined.astype(jnp.bfloat16).reshape(o_ref.shape)


def attend_time(halfway, modulation, wide_weights, weights, into, total_per, place):
    devices, frames, per, features = halfway.shape
    block = min(16, per)
    rows = devices * frames * block
    start = place // block
    operands = [halfway, modulation, wide_weights, weights]
    in_specs = [
        pl.BlockSpec((devices, frames, block, features), lambda s: (0, 0, s, 0)),
        pl.BlockSpec(modulation.shape, lambda s: (0, 0)),
        pl.BlockSpec(wide_weights.shape, lambda s: (0, 0), pipeline_mode=pl.Buffered(1)),
        pl.BlockSpec(weights.shape, lambda s: (0, 0), pipeline_mode=pl.Buffered(1)),
    ]
    aliases = {}
    if into is not None:
        operands.append(into)
        in_specs.append(pl.BlockSpec(memory_space=pl.ANY))
        aliases = {4: 0}
    return pl.pallas_call(
        time_kernel,
        out_shape=jax.ShapeDtypeStruct((devices, frames, total_per, features), jnp.bfloat16),
        grid=(per // block,),
        in_specs=in_specs,
        out_specs=pl.BlockSpec(
            (devices, frames, block, features), lambda s: (0, 0, start + s, 0)
        ),
        scratch_shapes=[
            pltpu.VMEM((rows, 3 * features), jnp.bfloat16),
            pltpu.VMEM((rows, features), jnp.float32),
        ],
        input_output_aliases=aliases,
        compiler_params=pltpu.CompilerParams(vmem_limit_bytes=VMEM_LIMIT),
        cost_estimate=pl.CostEstimate(
            flops=2
            * halfway.size
            * (4 * features + 2 * 8 * devices * frames * HEADS * WINDOW // features),
            bytes_accessed=4 * halfway.size + 8 * features * features,
            transcendentals=halfway.size // features * 8 * devices * frames * HEADS,
        ),
        name="time_block",
    )(*operands)


def place_kernel(x_ref, *rest):
    o_ref = rest[-1]
    owners, frames, per, features = x_ref.shape
    for frame in range(frames):
        o_ref[frame] = x_ref[:, frame].reshape(owners * per, features)


def place_sites(piece, into, shape, slot, per, first):
    owners, frames, _, features = piece.shape
    block = 4
    operands = [piece]
    in_specs = [
        pl.BlockSpec((block, frames, per, features), lambda d: (d, 0, slot // per, 0))
    ]
    aliases = {}
    if into is not None:
        operands.append(into)
        in_specs.append(pl.BlockSpec(memory_space=pl.ANY))
        aliases = {1: 0}
    start = first // (block * per)
    return pl.pallas_call(
        place_kernel,
        out_shape=jax.ShapeDtypeStruct(shape, jnp.bfloat16),
        grid=(owners // block,),
        in_specs=in_specs,
        out_specs=pl.BlockSpec((frames, block * per, features), lambda d: (0, start + d, 0)),
        input_output_aliases=aliases,
        compiler_params=pltpu.CompilerParams(vmem_limit_bytes=VMEM_LIMIT),
        cost_estimate=pl.CostEstimate(
            flops=0,
            bytes_accessed=4 * owners * frames * per * features,
            transcendentals=0,
        ),
        name="place_sites",
    )(*operands)


def exchange(pieces):
    return lax.all_to_all(pieces, "wide", split_axis=0, concat_axis=0, tiled=True)


def on_device(video, modulation, spatial_input, spatial_output, temporal_input, temporal_output):
    frames, sites, features = video.shape
    devices = lax.axis_size("wide")
    triples = project_space(video, modulation, spatial_input)
    unit = sites // sum(FORWARD)
    first = 0
    arrived = []
    for share in FORWARD:
        count = share * unit
        halfway = attend_space(
            video, triples, modulation, spatial_output, first, count, devices
        )
        arrived.append(exchange(halfway))
        first += count
    refined = None
    first = 0
    for members in BACKWARD:
        total_per = sum(arrived[m].shape[2] for m in members)
        done, place = None, 0
        for m in members:
            done = attend_time(
                arrived[m], modulation, temporal_input, temporal_output, done, total_per, place
            )
            place += arrived[m].shape[2]
        back = exchange(done)
        place = 0
        for m in members:
            per = arrived[m].shape[2]
            refined = place_sites(back, refined, video.shape, place, per, first)
            place += per
            first += per * devices
    return refined


def solution(mesh):
    placed = (P(("groups", "wide"), None, None), P("groups", None), P(), P(), P(), P())
    return jax.shard_map(
        on_device,
        mesh=mesh,
        in_specs=placed,
        out_specs=P(("groups", "wide"), None, None),
        check_vma=False,
    )
```

```python
import functools
import math

import jax
import jax.numpy as jnp
from jax import lax
from jax.experimental import pallas as pl
from jax.experimental.pallas import tpu as pltpu
from jax.sharding import PartitionSpec as P

HEADS = 16
HEAD_DIM = 72
EPSILON = 1e-06
SCORE_SCALE = math.log2(math.e) / math.sqrt(HEAD_DIM)
LANES = 128
WINDOW = 2 * LANES
FAR = -1e30
VMEM_LIMIT = 63 * 1024 * 1024
BLOCKS = 4
RETURNS = ((0, 1), (2, 3))
HEADS_AT_ONCE = 4


def departures(frames):
    if frames == 2:
        return (((0, 0), (0, 1), (0, 2)), ((1, 0), (1, 1)), ((0, 3), (1, 2), (1, 3)))
    whole = [tuple((frame, block) for frame in range(frames)) for block in range(BLOCKS)]
    return (whole[0], whole[1], whole[2] + whole[3])


def pick(step, values):
    chosen = values[0]
    for index in range(1, len(values)):
        chosen = jnp.where(step == index, values[index], chosen)
    return chosen


def normalize(values, offset_row, stretch):
    average = jnp.mean(values, axis=-1, keepdims=True)
    centered = values - average
    spread = jnp.mean(centered * centered, axis=-1, keepdims=True)
    return (centered * lax.rsqrt(spread + EPSILON) * (1.0 + stretch) + offset_row).astype(
        jnp.bfloat16
    )


def head_window(head, features):
    last = features // LANES - 2
    if isinstance(head, int):
        tile = min(head * HEAD_DIM // LANES, last)
        return tile * LANES, head * HEAD_DIM - tile * LANES
    tile = jnp.minimum(head * HEAD_DIM // LANES, last)
    return pl.multiple_of(tile * LANES, LANES), head * HEAD_DIM - tile * LANES


def attend_head(head, q_of, k_of, v_of, total, rows, features, allowed=None):
    lane, first = head_window(head, features)
    lanes = lax.broadcasted_iota(jnp.int32, (rows.size, WINDOW), 1)
    mine = (lanes >= first) & (lanes < first + HEAD_DIM)
    scores = lax.dot_general(
        jnp.where(mine, q_of(lane), 0),
        k_of(lane),
        (((1,), (1,)), ((), ())),
        preferred_element_type=jnp.float32,
    )
    if allowed is not None:
        scores = jnp.where(allowed, scores, FAR)
    largest = jnp.max(scores, axis=-1, keepdims=True)
    powers = jnp.exp2(scores - largest)
    weight = jnp.sum(powers, axis=-1, keepdims=True)
    mixed = jnp.dot(powers.astype(jnp.bfloat16), v_of(lane), preferred_element_type=jnp.float32)
    mixed = jnp.where(mine, mixed * (1.0 / weight), 0.0)
    total[rows, pl.ds(lane, WINDOW)] = total[rows, pl.ds(lane, WINDOW)] + mixed


def project_space_kernel(x_ref, mod_ref, w_ref, *rest):
    o_ref = rest[-1]
    features = x_ref.shape[1]
    normed = normalize(x_ref[...].astype(jnp.float32), mod_ref[0:1, :], mod_ref[1:2, :])
    product = jnp.dot(normed, w_ref[...], preferred_element_type=jnp.float32)
    o_ref[:, :features] = (product[:, :features] * SCORE_SCALE).astype(jnp.bfloat16)
    o_ref[:, features:] = product[:, features:].astype(jnp.bfloat16)


def project_space(video, frame, modulation, weights, into):
    frames, sites, features = video.shape
    block = 128
    first = frame * (sites // block)
    operands = [video.reshape(-1, features), modulation, weights]
    in_specs = [
        pl.BlockSpec((block, features), lambda r: (first + r, 0)),
        pl.BlockSpec(modulation.shape, lambda r: (0, 0)),
        pl.BlockSpec(weights.shape, lambda r: (0, 0), pipeline_mode=pl.Buffered(1)),
    ]
    aliases = {}
    if into is not None:
        operands.append(into)
        in_specs.append(pl.BlockSpec(memory_space=pl.ANY))
        aliases = {3: 0}
    return pl.pallas_call(
        project_space_kernel,
        out_shape=jax.ShapeDtypeStruct((frames * sites, 3 * features), jnp.bfloat16),
        grid=(sites // block,),
        in_specs=in_specs,
        out_specs=pl.BlockSpec((block, 3 * features), lambda r: (first + r, 0)),
        input_output_aliases=aliases,
        compiler_params=pltpu.CompilerParams(vmem_limit_bytes=VMEM_LIMIT),
        cost_estimate=pl.CostEstimate(
            flops=2 * sites * features * 3 * features,
            bytes_accessed=2 * (4 * sites * features + 3 * features * features),
            transcendentals=0,
        ),
        name="space_project",
    )(*operands)


def attend_space_kernel(x_ref, q_ref, k_ref, v_ref, mod_ref, w_ref, o_ref, total):
    rows, features = q_ref.shape
    total[...] = jnp.zeros_like(total)
    for head in range(HEADS):
        attend_head(
            head,
            lambda lane: q_ref[:, pl.ds(lane, WINDOW)],
            lambda lane: k_ref[:, pl.ds(lane, WINDOW)],
            lambda lane: v_ref[:, pl.ds(lane, WINDOW)],
            total,
            pl.ds(0, rows),
            features,
        )
    branch = jnp.dot(
        total[...].astype(jnp.bfloat16), w_ref[...], preferred_element_type=jnp.float32
    )
    halfway = x_ref[0].astype(jnp.float32) + mod_ref[2:3, :] * branch
    o_ref[...] = halfway.astype(jnp.bfloat16).reshape(o_ref.shape)


def attend_space(video, triples, modulation, weights, group, devices):
    _, sites, features = video.shape
    block = sites // BLOCKS
    per = block // devices
    count = len(group)

    def frame(s):
        return pick(s, [f for f, _ in group])

    def place(s):
        return pick(s, [b for _, b in group])

    return pl.pallas_call(
        attend_space_kernel,
        out_shape=jax.ShapeDtypeStruct((devices, count, per, features), jnp.bfloat16),
        grid=(count,),
        in_specs=[
            pl.BlockSpec((1, block, features), lambda s: (frame(s), place(s), 0)),
            pl.BlockSpec((block, features), lambda s: (frame(s) * BLOCKS + place(s), 0)),
            pl.BlockSpec((sites, features), lambda s: (frame(s), 1)),
            pl.BlockSpec((sites, features), lambda s: (frame(s), 2)),
            pl.BlockSpec(modulation.shape, lambda s: (0, 0)),
            pl.BlockSpec(weights.shape, lambda s: (0, 0)),
        ],
        out_specs=pl.BlockSpec((devices, 1, per, features), lambda s: (0, s, 0, 0)),
        scratch_shapes=[pltpu.VMEM((block, features), jnp.float32)],
        compiler_params=pltpu.CompilerParams(vmem_limit_bytes=VMEM_LIMIT),
        cost_estimate=pl.CostEstimate(
            flops=2 * count * block * (features * features + 2 * sites * HEADS * WINDOW),
            bytes_accessed=2 * features * (3 * count * block + 2 * sites + features),
            transcendentals=count * block * sites * HEADS,
        ),
        name="space_attend",
    )(video, triples, triples, triples, modulation, weights)


def time_kernel(sources, mod_ref, wi_ref, wo_ref, *rest):
    o_ref, stream, triples, total = rest[-4:]
    step = pl.program_id(0)
    devices, frames, per, features = o_ref.shape
    groups = per // 8
    size = devices * frames * 8
    share = devices * 8
    for frame, refs in enumerate(sources):
        arrived = pick(step, [rest[index][:, 0] for index in refs]).astype(jnp.float32)
        for g in range(groups):
            stream[pl.ds(g * size + frame * share, share), :] = arrived[
                :, 8 * g : 8 * g + 8, :
            ].reshape(share, features)
    site_of_query = lax.broadcasted_iota(jnp.int32, (size, size), 0) % 8
    site_of_key = lax.broadcasted_iota(jnp.int32, (size, size), 1) % 8

    def one_group(g, carry):
        here = pl.ds(pl.multiple_of(g * size, size), size)
        normed = normalize(stream[here, :], mod_ref[3:4, :], mod_ref[4:5, :])
        product = jnp.dot(normed, wi_ref[...], preferred_element_type=jnp.float32)
        triples[:, :features] = (product[:, :features] * SCORE_SCALE).astype(jnp.bfloat16)
        triples[:, features:] = product[:, features:].astype(jnp.bfloat16)
        total[...] = jnp.zeros_like(total)

        def one_head(head, carry):
            attend_head(
                head,
                lambda lane: triples[:, pl.ds(lane, WINDOW)],
                lambda lane: triples[:, pl.ds(pl.multiple_of(features + lane, LANES), WINDOW)],
                lambda lane: triples[:, pl.ds(pl.multiple_of(2 * features + lane, LANES), WINDOW)],
                total,
                pl.ds(0, size),
                features,
                site_of_query == site_of_key,
            )
            return carry

        lax.fori_loop(0, HEADS, one_head, 0, unroll=HEADS_AT_ONCE)
        branch = jnp.dot(
            total[...].astype(jnp.bfloat16), wo_ref[...], preferred_element_type=jnp.float32
        )
        stream[here, :] = stream[here, :] + mod_ref[5:6, :] * branch
        return carry

    lax.fori_loop(0, groups, one_group, 0)
    for frame in range(frames):
        o_ref[:, frame] = jnp.concatenate(
            [
                stream[pl.ds(g * size + frame * share, share), :].reshape(devices, 8, features)
                for g in range(groups)
            ],
            axis=1,
        ).astype(jnp.bfloat16)


def attend_time(arrived, blocks, frames, modulation, wide_weights, weights):
    operands = [modulation, wide_weights, weights]
    in_specs = [
        pl.BlockSpec(modulation.shape, lambda s: (0, 0)),
        pl.BlockSpec(wide_weights.shape, lambda s: (0, 0), pipeline_mode=pl.Buffered(1)),
        pl.BlockSpec(weights.shape, lambda s: (0, 0), pipeline_mode=pl.Buffered(1)),
    ]
    sources = []
    for frame in range(frames):
        arrays, slots, refs = [], [], []
        for block in blocks:
            array, slot = arrived[frame, block]
            known = [index for index, other in enumerate(arrays) if other is array]
            if not known:
                known = [len(arrays)]
                arrays.append(array)
                slots.append([])
            slots[known[0]].append(slot)
            refs.append(len(operands) - 3 + known[0])
        for array, places in zip(arrays, slots):
            devices, _, per, features = array.shape
            in_specs.append(
                pl.BlockSpec(
                    (devices, 1, per, features),
                    lambda s, places=places: (
                        0,
                        pick(s, places) if len(places) > 1 else places[0],
                        0,
                        0,
                    ),
                )
            )
            operands.append(array)
        sources.append(refs if len(arrays) > 1 else refs[:1])
    rows = devices * frames * per
    size = devices * frames * 8
    return pl.pallas_call(
        functools.partial(time_kernel, sources),
        out_shape=jax.ShapeDtypeStruct(
            (devices, frames, len(blocks) * per, features), jnp.bfloat16
        ),
        grid=(len(blocks),),
        in_specs=in_specs,
        out_specs=pl.BlockSpec((devices, frames, per, features), lambda s: (0, 0, s, 0)),
        scratch_shapes=[
            pltpu.VMEM((rows, features), jnp.float32),
            pltpu.VMEM((size, 3 * features), jnp.bfloat16),
            pltpu.VMEM((size, features), jnp.float32),
        ],
        compiler_params=pltpu.CompilerParams(vmem_limit_bytes=VMEM_LIMIT),
        cost_estimate=pl.CostEstimate(
            flops=len(blocks)
            * (
                2 * rows * features * 4 * features
                + 4 * rows * 8 * devices * frames * HEADS * WINDOW
            ),
            bytes_accessed=len(blocks) * 4 * rows * features + 8 * features * features,
            transcendentals=len(blocks) * rows * 8 * devices * frames * HEADS,
        ),
        name="time_block",
    )(*operands)


def place_sites(piece, into, first, count):
    owners, frames, sites, features = piece.shape
    per = sites // count
    stage = owners // 4

    def place_kernel(x_hbm, *rest):
        o_hbm, held, arriving, leaving = rest[-4:]
        inward = [
            pltpu.make_async_copy(
                x_hbm.at[pl.ds(low, stage)], held.at[pl.ds(low, stage)], arriving.at[index]
            )
            for index, low in enumerate(range(0, owners, stage))
        ]
        for copy in inward:
            copy.start()
        outward = []
        for index, low in enumerate(range(0, owners, stage)):
            inward[index].wait()
            for frame in range(frames):
                for block in range(count):
                    outward.append(
                        pltpu.make_async_copy(
                            held.at[pl.ds(low, stage), frame, pl.ds(block * per, per)],
                            o_hbm.at[frame, pl.ds((first + block) * owners + low, stage)],
                            leaving.at[len(outward)],
                        )
                    )
                    outward[-1].start()
        for copy in outward:
            copy.wait()

    operands = [piece]
    aliases = {}
    if into is not None:
        operands.append(into)
        aliases = {1: 0}
    return pl.pallas_call(
        place_kernel,
        out_shape=jax.ShapeDtypeStruct((frames, BLOCKS * owners, per, features), jnp.bfloat16),
        in_specs=[pl.BlockSpec(memory_space=pl.ANY)] * len(operands),
        out_specs=pl.BlockSpec(memory_space=pl.ANY),
        scratch_shapes=[
            pltpu.VMEM(piece.shape, jnp.bfloat16),
            pltpu.SemaphoreType.DMA((4,)),
            pltpu.SemaphoreType.DMA((4 * frames * count,)),
        ],
        input_output_aliases=aliases,
        compiler_params=pltpu.CompilerParams(vmem_limit_bytes=VMEM_LIMIT),
        cost_estimate=pl.CostEstimate(
            flops=0, bytes_accessed=4 * piece.size, transcendentals=0
        ),
        name="place_sites",
    )(*operands)


def exchange(pieces, earlier):
    if earlier is not None:
        pieces, earlier = lax.optimization_barrier((pieces, earlier))
    return lax.all_to_all(pieces, "wide", split_axis=0, concat_axis=0, tiled=True), earlier


def on_device(video, modulation, spatial_input, spatial_output, temporal_input, temporal_output):
    frames, sites, features = video.shape
    devices = lax.axis_size("wide")
    triples = None
    projected = set()
    landings = []
    arrived = {}
    landed = None
    for group in departures(frames):
        for frame in sorted({frame for frame, _ in group} - projected):
            triples = project_space(video, frame, modulation, spatial_input, triples)
            projected.add(frame)
        leaving = attend_space(video, triples, modulation, spatial_output, group, devices)
        leaving, triples = lax.optimization_barrier((leaving, triples))
        landed, earlier = exchange(leaving, landed)
        landings[-1:] = [earlier, landed] if landings else [landed]
        for slot, pair in enumerate(group):
            arrived[pair] = len(landings) - 1, slot
    refined = None
    for blocks in RETURNS:
        done = attend_time(
            {pair: (landings[index], slot) for pair, (index, slot) in arrived.items()},
            blocks,
            frames,
            modulation,
            temporal_input,
            temporal_output,
        )
        last = landed is landings[-1]
        landed, earlier = exchange(done, landed)
        if last:
            landings[-1] = earlier
        else:
            back = earlier
            refined = place_sites(back, refined, previous[0], len(previous))
        previous = blocks
    refined = place_sites(landed, refined, previous[0], len(previous))
    return refined.reshape(video.shape)


def solution(mesh):
    placed = (P(("groups", "wide"), None, None), P("groups", None), P(), P(), P(), P())
    return jax.shard_map(
        on_device,
        mesh=mesh,
        in_specs=placed,
        out_specs=P(("groups", "wide"), None, None),
        check_vma=False,
    )
```

```python
import functools
import math

import jax
import jax.numpy as jnp
from jax import lax
from jax.experimental import pallas as pl
from jax.experimental.pallas import tpu as pltpu
from jax.sharding import PartitionSpec as P

HEADS = 16
HEAD_DIM = 72
EPSILON = 1e-06
SCORE_SCALE = math.log2(math.e) / math.sqrt(HEAD_DIM)
LANES = 128
WINDOW = 2 * LANES
FAR = -1e30
VMEM_LIMIT = 63 * 1024 * 1024
BLOCKS = 4
RETURNS = ((0, 1), (2, 3))
HEADS_AT_ONCE = 4


def departures(frames):
    if frames == 2:
        return (((0, 0), (0, 1)), ((1, 0), (1, 1)), ((0, 2), (0, 3), (1, 2), (1, 3)))
    whole = [tuple((frame, block) for frame in range(frames)) for block in range(BLOCKS)]
    return (whole[0], whole[1], whole[2] + whole[3])


def pick(step, values):
    chosen = values[0]
    for index in range(1, len(values)):
        chosen = jnp.where(step == index, values[index], chosen)
    return chosen


def normalize(values, offset_row, stretch):
    average = jnp.mean(values, axis=-1, keepdims=True)
    centered = values - average
    spread = jnp.mean(centered * centered, axis=-1, keepdims=True)
    return (centered * lax.rsqrt(spread + EPSILON) * (1.0 + stretch) + offset_row).astype(
        jnp.bfloat16
    )


def head_window(head, features):
    last = features // LANES - 2
    if isinstance(head, int):
        tile = min(head * HEAD_DIM // LANES, last)
        return tile * LANES, head * HEAD_DIM - tile * LANES
    tile = jnp.minimum(head * HEAD_DIM // LANES, last)
    return pl.multiple_of(tile * LANES, LANES), head * HEAD_DIM - tile * LANES


def attend_head(head, q_of, k_of, v_of, total, rows, features, allowed=None):
    lane, first = head_window(head, features)
    lanes = lax.broadcasted_iota(jnp.int32, (rows.size, WINDOW), 1)
    mine = (lanes >= first) & (lanes < first + HEAD_DIM)
    scores = lax.dot_general(
        jnp.where(mine, q_of(lane), 0),
        k_of(lane),
        (((1,), (1,)), ((), ())),
        preferred_element_type=jnp.float32,
    )
    if allowed is not None:
        scores = jnp.where(allowed, scores, FAR)
    largest = jnp.max(scores, axis=-1, keepdims=True)
    powers = jnp.exp2(scores - largest)
    weight = jnp.sum(powers, axis=-1, keepdims=True)
    mixed = jnp.dot(powers.astype(jnp.bfloat16), v_of(lane), preferred_element_type=jnp.float32)
    mixed = jnp.where(mine, mixed * (1.0 / weight), 0.0)
    total[rows, pl.ds(lane, WINDOW)] = total[rows, pl.ds(lane, WINDOW)] + mixed


def attend_heads(q_of, k_of, v_of, total, x_ref, mod_ref, w_ref, o_ref):
    rows, features = total.shape
    total[...] = jnp.zeros_like(total)
    for head in range(HEADS):
        attend_head(head, q_of, k_of, v_of, total, pl.ds(0, rows), features)
    branch = jnp.dot(
        total[...].astype(jnp.bfloat16), w_ref[...], preferred_element_type=jnp.float32
    )
    halfway = x_ref[0].astype(jnp.float32) + mod_ref[2:3, :] * branch
    o_ref[...] = halfway.astype(jnp.bfloat16).reshape(o_ref.shape)


def project(values, mod_ref, row, w_ref, target, rows):
    features = values.shape[1]
    normed = normalize(values, mod_ref[row : row + 1, :], mod_ref[row + 1 : row + 2, :])
    product = jnp.dot(normed, w_ref[...], preferred_element_type=jnp.float32)
    target[rows, :features] = (product[:, :features] * SCORE_SCALE).astype(jnp.bfloat16)
    target[rows, features:] = product[:, features:].astype(jnp.bfloat16)


def open_space_kernel(frame, blocks, x_ref, mod_ref, wi_ref, wo_hbm, *rest):
    o_ref, t_hbm, triples, total, wo_ref, semaphores = rest[-6:]
    step = pl.program_id(0)
    _, rows, features = x_ref.shape
    sites = triples.shape[0]
    count = sites // rows

    def keep(block):
        here = pl.ds(pl.multiple_of(block * rows, rows), rows)
        there = pl.ds(pl.multiple_of(frame * sites + block * rows, rows), rows)
        return pltpu.make_async_copy(triples.at[here], t_hbm.at[there], semaphores.at[block])

    fetch = pltpu.make_async_copy(wo_hbm, wo_ref, semaphores.at[count])
    pl.when(step == 0)(fetch.start)
    pl.when(step == count)(fetch.wait)

    @pl.when(step < count)
    def _():
        here = pl.ds(pl.multiple_of(step * rows, rows), rows)
        project(x_ref[0].astype(jnp.float32), mod_ref, 0, wi_ref, triples, here)
        keep(step).start()

    @pl.when(step >= count)
    def _():
        first = pl.multiple_of(pick(step - count, blocks) * rows, rows)
        attend_heads(
            lambda lane: triples[pl.ds(first, rows), pl.ds(lane, WINDOW)],
            lambda lane: triples[:, pl.ds(features + lane, WINDOW)],
            lambda lane: triples[:, pl.ds(2 * features + lane, WINDOW)],
            total,
            x_ref,
            mod_ref,
            wo_ref,
            o_ref,
        )

    @pl.when(step == count + len(blocks) - 1)
    def _():
        for block in range(count):
            keep(block).wait()


def open_space(video, modulation, wide_weights, weights, frame, blocks, into, devices):
    frames, sites, features = video.shape
    block = sites // BLOCKS
    per = block // devices
    operands = [video, modulation, wide_weights, weights]
    in_specs = [
        pl.BlockSpec(
            (1, block, features),
            lambda s: (frame, jnp.where(s < BLOCKS, s, pick(s - BLOCKS, blocks)), 0),
        ),
        pl.BlockSpec(modulation.shape, lambda s: (0, 0)),
        pl.BlockSpec(wide_weights.shape, lambda s: (0, 0), pipeline_mode=pl.Buffered(1)),
        pl.BlockSpec(memory_space=pl.ANY),
    ]
    aliases = {}
    if into is not None:
        operands.append(into)
        in_specs.append(pl.BlockSpec(memory_space=pl.ANY))
        aliases = {4: 1}
    count = len(blocks)
    return pl.pallas_call(
        functools.partial(open_space_kernel, frame, blocks),
        out_shape=[
            jax.ShapeDtypeStruct((devices, count, per, features), jnp.bfloat16),
            jax.ShapeDtypeStruct((frames * sites, 3 * features), jnp.bfloat16),
        ],
        grid=(BLOCKS + count,),
        in_specs=in_specs,
        out_specs=[
            pl.BlockSpec(
                (devices, 1, per, features), lambda s: (0, jnp.maximum(s - BLOCKS, 0), 0, 0)
            ),
            pl.BlockSpec(memory_space=pl.ANY),
        ],
        scratch_shapes=[
            pltpu.VMEM((sites, 3 * features), jnp.bfloat16),
            pltpu.VMEM((block, features), jnp.float32),
            pltpu.VMEM(weights.shape, jnp.bfloat16),
            pltpu.SemaphoreType.DMA((BLOCKS + 1,)),
        ],
        input_output_aliases=aliases,
        compiler_params=pltpu.CompilerParams(vmem_limit_bytes=VMEM_LIMIT),
        cost_estimate=pl.CostEstimate(
            flops=2 * sites * features * 3 * features
            + 2 * count * block * (features * features + 2 * sites * HEADS * WINDOW),
            bytes_accessed=2 * features * (4 * sites + 2 * count * block + 4 * features),
            transcendentals=count * block * sites * HEADS,
        ),
        name="space_open",
    )(*operands)


def attend_space_kernel(x_ref, q_ref, k_ref, v_ref, mod_ref, w_ref, o_ref, total):
    attend_heads(
        lambda lane: q_ref[:, pl.ds(lane, WINDOW)],
        lambda lane: k_ref[:, pl.ds(lane, WINDOW)],
        lambda lane: v_ref[:, pl.ds(lane, WINDOW)],
        total,
        x_ref,
        mod_ref,
        w_ref,
        o_ref,
    )


def attend_space(video, triples, modulation, weights, group, devices):
    _, sites, features = video.shape
    block = sites // BLOCKS
    per = block // devices
    count = len(group)

    def frame(s):
        return pick(s, [f for f, _ in group])

    def place(s):
        return pick(s, [b for _, b in group])

    return pl.pallas_call(
        attend_space_kernel,
        out_shape=jax.ShapeDtypeStruct((devices, count, per, features), jnp.bfloat16),
        grid=(count,),
        in_specs=[
            pl.BlockSpec((1, block, features), lambda s: (frame(s), place(s), 0)),
            pl.BlockSpec((block, features), lambda s: (frame(s) * BLOCKS + place(s), 0)),
            pl.BlockSpec((sites, features), lambda s: (frame(s), 1)),
            pl.BlockSpec((sites, features), lambda s: (frame(s), 2)),
            pl.BlockSpec(modulation.shape, lambda s: (0, 0)),
            pl.BlockSpec(weights.shape, lambda s: (0, 0)),
        ],
        out_specs=pl.BlockSpec((devices, 1, per, features), lambda s: (0, s, 0, 0)),
        scratch_shapes=[pltpu.VMEM((block, features), jnp.float32)],
        compiler_params=pltpu.CompilerParams(vmem_limit_bytes=VMEM_LIMIT),
        cost_estimate=pl.CostEstimate(
            flops=2 * count * block * (features * features + 2 * sites * HEADS * WINDOW),
            bytes_accessed=2 * features * (3 * count * block + 2 * sites + features),
            transcendentals=count * block * sites * HEADS,
        ),
        name="space_attend",
    )(video, triples, triples, triples, modulation, weights)


def time_kernel(sources, mod_ref, wi_ref, wo_ref, *rest):
    o_ref, stream, triples, total = rest[-4:]
    step = pl.program_id(0)
    devices, frames, per, features = o_ref.shape
    groups = per // 8
    size = devices * frames * 8
    share = devices * 8
    for frame, refs in enumerate(sources):
        arrived = pick(step, [rest[index][:, 0] for index in refs]).astype(jnp.float32)
        for g in range(groups):
            stream[pl.ds(g * size + frame * share, share), :] = arrived[
                :, 8 * g : 8 * g + 8, :
            ].reshape(share, features)
    site_of_query = lax.broadcasted_iota(jnp.int32, (size, size), 0) % 8
    site_of_key = lax.broadcasted_iota(jnp.int32, (size, size), 1) % 8

    def one_group(g, carry):
        here = pl.ds(pl.multiple_of(g * size, size), size)
        half = size // 2

        def one_half(h, carry):
            start = pl.multiple_of(h * half, half)
            values = stream[pl.ds(pl.multiple_of(g * size + start, half), half), :]
            project(values, mod_ref, 3, wi_ref, triples, pl.ds(start, half))
            return carry

        lax.fori_loop(0, 2, one_half, 0)
        total[...] = jnp.zeros_like(total)

        def one_head(head, carry):
            attend_head(
                head,
                lambda lane: triples[:, pl.ds(lane, WINDOW)],
                lambda lane: triples[:, pl.ds(pl.multiple_of(features + lane, LANES), WINDOW)],
                lambda lane: triples[:, pl.ds(pl.multiple_of(2 * features + lane, LANES), WINDOW)],
                total,
                pl.ds(0, size),
                features,
                site_of_query == site_of_key,
            )
            return carry

        lax.fori_loop(0, HEADS, one_head, 0, unroll=HEADS_AT_ONCE)
        branch = jnp.dot(
            total[...].astype(jnp.bfloat16), wo_ref[...], preferred_element_type=jnp.float32
        )
        stream[here, :] = stream[here, :] + mod_ref[5:6, :] * branch
        return carry

    lax.fori_loop(0, groups, one_group, 0)
    for frame in range(frames):
        o_ref[:, frame] = jnp.concatenate(
            [
                stream[pl.ds(g * size + frame * share, share), :].reshape(devices, 8, features)
                for g in range(groups)
            ],
            axis=1,
        ).astype(jnp.bfloat16)


def attend_time(arrived, blocks, frames, modulation, wide_weights, weights):
    operands = [modulation, wide_weights, weights]
    in_specs = [
        pl.BlockSpec(modulation.shape, lambda s: (0, 0)),
        pl.BlockSpec(wide_weights.shape, lambda s: (0, 0), pipeline_mode=pl.Buffered(1)),
        pl.BlockSpec(weights.shape, lambda s: (0, 0), pipeline_mode=pl.Buffered(1)),
    ]
    sources = []
    for frame in range(frames):
        arrays, slots, refs = [], [], []
        for block in blocks:
            array, slot = arrived[frame, block]
            known = [index for index, other in enumerate(arrays) if other is array]
            if not known:
                known = [len(arrays)]
                arrays.append(array)
                slots.append([])
            slots[known[0]].append(slot)
            refs.append(len(operands) - 3 + known[0])
        for array, places in zip(arrays, slots):
            devices, _, per, features = array.shape
            in_specs.append(
                pl.BlockSpec(
                    (devices, 1, per, features),
                    lambda s, places=places: (
                        0,
                        pick(s, places) if len(places) > 1 else places[0],
                        0,
                        0,
                    ),
                )
            )
            operands.append(array)
        sources.append(refs if len(arrays) > 1 else refs[:1])
    rows = devices * frames * per
    size = devices * frames * 8
    return pl.pallas_call(
        functools.partial(time_kernel, sources),
        out_shape=jax.ShapeDtypeStruct(
            (devices, frames, len(blocks) * per, features), jnp.bfloat16
        ),
        grid=(len(blocks),),
        in_specs=in_specs,
        out_specs=pl.BlockSpec((devices, frames, per, features), lambda s: (0, 0, s, 0)),
        scratch_shapes=[
            pltpu.VMEM((rows, features), jnp.float32),
            pltpu.VMEM((size, 3 * features), jnp.bfloat16),
            pltpu.VMEM((size, features), jnp.float32),
        ],
        compiler_params=pltpu.CompilerParams(vmem_limit_bytes=VMEM_LIMIT),
        cost_estimate=pl.CostEstimate(
            flops=len(blocks)
            * (
                2 * rows * features * 4 * features
                + 4 * rows * 8 * devices * frames * HEADS * WINDOW
            ),
            bytes_accessed=len(blocks) * 4 * rows * features + 8 * features * features,
            transcendentals=len(blocks) * rows * 8 * devices * frames * HEADS,
        ),
        name="time_block",
    )(*operands)


def place_sites(piece, into, first, count):
    owners, frames, sites, features = piece.shape
    per = sites // count
    stage = owners // 4

    def place_kernel(x_hbm, *rest):
        o_hbm, held, arriving, leaving = rest[-4:]
        inward = [
            pltpu.make_async_copy(
                x_hbm.at[pl.ds(low, stage)], held.at[pl.ds(low, stage)], arriving.at[index]
            )
            for index, low in enumerate(range(0, owners, stage))
        ]
        for copy in inward:
            copy.start()
        outward = []
        for index, low in enumerate(range(0, owners, stage)):
            inward[index].wait()
            for frame in range(frames):
                for block in range(count):
                    outward.append(
                        pltpu.make_async_copy(
                            held.at[pl.ds(low, stage), frame, pl.ds(block * per, per)],
                            o_hbm.at[frame, pl.ds((first + block) * owners + low, stage)],
                            leaving.at[len(outward)],
                        )
                    )
                    outward[-1].start()
        for copy in outward:
            copy.wait()

    operands = [piece]
    aliases = {}
    if into is not None:
        operands.append(into)
        aliases = {1: 0}
    return pl.pallas_call(
        place_kernel,
        out_shape=jax.ShapeDtypeStruct((frames, BLOCKS * owners, per, features), jnp.bfloat16),
        in_specs=[pl.BlockSpec(memory_space=pl.ANY)] * len(operands),
        out_specs=pl.BlockSpec(memory_space=pl.ANY),
        scratch_shapes=[
            pltpu.VMEM(piece.shape, jnp.bfloat16),
            pltpu.SemaphoreType.DMA((4,)),
            pltpu.SemaphoreType.DMA((4 * frames * count,)),
        ],
        input_output_aliases=aliases,
        compiler_params=pltpu.CompilerParams(vmem_limit_bytes=VMEM_LIMIT),
        cost_estimate=pl.CostEstimate(
            flops=0, bytes_accessed=4 * piece.size, transcendentals=0
        ),
        name="place_sites",
    )(*operands)


def exchange(pieces, earlier):
    if earlier is not None:
        pieces, earlier = lax.optimization_barrier((pieces, earlier))
    return lax.all_to_all(pieces, "wide", split_axis=0, concat_axis=0, tiled=True), earlier


def on_device(video, modulation, spatial_input, spatial_output, temporal_input, temporal_output):
    frames, sites, features = video.shape
    devices = lax.axis_size("wide")
    triples = None
    opened = set()
    landings = []
    arrived = {}
    landed = None
    for group in departures(frames):
        fresh = sorted({frame for frame, _ in group} - opened)
        if len(fresh) == 1 and {frame for frame, _ in group} == set(fresh):
            leaving, triples = open_space(
                video,
                modulation,
                spatial_input,
                spatial_output,
                fresh[0],
                [block for _, block in group],
                triples,
                devices,
            )
            opened.update(fresh)
        else:
            leaving = attend_space(video, triples, modulation, spatial_output, group, devices)
        leaving, triples = lax.optimization_barrier((leaving, triples))
        landed, earlier = exchange(leaving, landed)
        landings[-1:] = [earlier, landed] if landings else [landed]
        for slot, pair in enumerate(group):
            arrived[pair] = len(landings) - 1, slot
    refined = None
    for blocks in RETURNS:
        done = attend_time(
            {pair: (landings[index], slot) for pair, (index, slot) in arrived.items()},
            blocks,
            frames,
            modulation,
            temporal_input,
            temporal_output,
        )
        last = landed is landings[-1]
        landed, earlier = exchange(done, landed)
        if last:
            landings[-1] = earlier
        else:
            back = earlier
            refined = place_sites(back, refined, previous[0], len(previous))
        previous = blocks
    refined = place_sites(landed, refined, previous[0], len(previous))
    return refined.reshape(video.shape)


def solution(mesh):
    placed = (P(("groups", "wide"), None, None), P("groups", None), P(), P(), P(), P())
    return jax.shard_map(
        on_device,
        mesh=mesh,
        in_specs=placed,
        out_specs=P(("groups", "wide"), None, None),
        check_vma=False,
    )
```

```python
import functools
import math

import jax
import jax.numpy as jnp
from jax import lax
from jax.experimental import pallas as pl
from jax.experimental.pallas import tpu as pltpu
from jax.sharding import PartitionSpec as P

HEADS = 16
HEAD_DIM = 72
EPSILON = 1e-06
SCORE_SCALE = math.log2(math.e) / math.sqrt(HEAD_DIM)
LANES = 128
WINDOW = 2 * LANES
FAR = -1e30
VMEM_LIMIT = 63 * 1024 * 1024
PLACE_LIMIT = 16 * 1024 * 1024
BLOCKS = 4
RETURNS = ((0, 1), (2, 3))
HEADS_AT_ONCE = 4


def departures(frames):
    if frames == 2:
        return (((0, 0), (0, 1)), ((1, 0), (1, 1)), ((0, 2), (0, 3), (1, 2), (1, 3)))
    whole = [tuple((frame, block) for frame in range(frames)) for block in range(BLOCKS)]
    return (whole[0], whole[1], whole[2] + whole[3])


def pick(step, values):
    chosen = values[0]
    for index in range(1, len(values)):
        chosen = jnp.where(step == index, values[index], chosen)
    return chosen


def normalize(values, offset_row, stretch):
    average = jnp.mean(values, axis=-1, keepdims=True)
    centered = values - average
    spread = jnp.mean(centered * centered, axis=-1, keepdims=True)
    return (centered * lax.rsqrt(spread + EPSILON) * (1.0 + stretch) + offset_row).astype(
        jnp.bfloat16
    )


def head_window(head, features):
    last = features // LANES - 2
    if isinstance(head, int):
        tile = min(head * HEAD_DIM // LANES, last)
        return tile * LANES, head * HEAD_DIM - tile * LANES
    tile = jnp.minimum(head * HEAD_DIM // LANES, last)
    return pl.multiple_of(tile * LANES, LANES), head * HEAD_DIM - tile * LANES


def in_head(rows, first):
    lanes = lax.broadcasted_iota(jnp.int32, (rows, WINDOW), 1)
    return (lanes >= first) & (lanes < first + HEAD_DIM)


def score_head(head, q_of, k_of, rows, features):
    lane, first = head_window(head, features)
    return lax.dot_general(
        jnp.where(in_head(rows, first), q_of(lane), 0),
        k_of(lane),
        (((1,), (1,)), ((), ())),
        preferred_element_type=jnp.float32,
    )


def mix_head(head, scores, v_of, total):
    rows, features = total.shape
    lane, first = head_window(head, features)
    largest = jnp.max(scores, axis=-1, keepdims=True)
    powers = jnp.exp2(scores - largest)
    weight = jnp.sum(powers, axis=-1, keepdims=True)
    mixed = jnp.dot(powers.astype(jnp.bfloat16), v_of(lane), preferred_element_type=jnp.float32)
    mixed = jnp.where(in_head(rows, first), mixed * (1.0 / weight), 0.0)
    total[:, pl.ds(lane, WINDOW)] = total[:, pl.ds(lane, WINDOW)] + mixed


def attend_heads(q_of, k_of, v_of, total, x_ref, mod_ref, w_ref, o_ref):
    rows, features = total.shape
    total[...] = jnp.zeros_like(total)
    scores = score_head(0, q_of, k_of, rows, features)
    for head in range(HEADS):
        following = None
        if head + 1 < HEADS:
            following = score_head(head + 1, q_of, k_of, rows, features)
        mix_head(head, scores, v_of, total)
        scores = following
    branch = jnp.dot(
        total[...].astype(jnp.bfloat16), w_ref[...], preferred_element_type=jnp.float32
    )
    halfway = x_ref[0].astype(jnp.float32) + mod_ref[2:3, :] * branch
    o_ref[...] = halfway.astype(jnp.bfloat16).reshape(o_ref.shape)


def project(values, mod_ref, row, w_ref, target, rows):
    features = values.shape[1]
    normed = normalize(values, mod_ref[row : row + 1, :], mod_ref[row + 1 : row + 2, :])
    product = jnp.dot(normed, w_ref[...], preferred_element_type=jnp.float32)
    target[rows, :features] = (product[:, :features] * SCORE_SCALE).astype(jnp.bfloat16)
    target[rows, features:] = product[:, features:].astype(jnp.bfloat16)


def open_space_kernel(frame, blocks, x_ref, mod_ref, wi_ref, wo_hbm, *rest):
    o_ref, t_hbm, triples, total, wo_ref, semaphores = rest[-6:]
    step = pl.program_id(0)
    _, rows, features = x_ref.shape
    sites = triples.shape[0]
    count = sites // rows

    def keep(block):
        here = pl.ds(pl.multiple_of(block * rows, rows), rows)
        there = pl.ds(pl.multiple_of(frame * sites + block * rows, rows), rows)
        return pltpu.make_async_copy(triples.at[here], t_hbm.at[there], semaphores.at[block])

    fetch = pltpu.make_async_copy(wo_hbm, wo_ref, semaphores.at[count])
    pl.when(step == 0)(fetch.start)
    pl.when(step == count)(fetch.wait)

    @pl.when(step < count)
    def _():
        here = pl.ds(pl.multiple_of(step * rows, rows), rows)
        project(x_ref[0].astype(jnp.float32), mod_ref, 0, wi_ref, triples, here)
        keep(step).start()

    @pl.when(step >= count)
    def _():
        first = pl.multiple_of(pick(step - count, blocks) * rows, rows)
        attend_heads(
            lambda lane: triples[pl.ds(first, rows), pl.ds(lane, WINDOW)],
            lambda lane: triples[:, pl.ds(features + lane, WINDOW)],
            lambda lane: triples[:, pl.ds(2 * features + lane, WINDOW)],
            total,
            x_ref,
            mod_ref,
            wo_ref,
            o_ref,
        )

    @pl.when(step == count + len(blocks) - 1)
    def _():
        for block in range(count):
            keep(block).wait()


def open_space(video, modulation, wide_weights, weights, frame, blocks, into, devices):
    frames, sites, features = video.shape
    block = sites // BLOCKS
    per = block // devices
    operands = [video, modulation, wide_weights, weights]
    in_specs = [
        pl.BlockSpec(
            (1, block, features),
            lambda s: (frame, jnp.where(s < BLOCKS, s, pick(s - BLOCKS, blocks)), 0),
        ),
        pl.BlockSpec(modulation.shape, lambda s: (0, 0)),
        pl.BlockSpec(wide_weights.shape, lambda s: (0, 0), pipeline_mode=pl.Buffered(1)),
        pl.BlockSpec(memory_space=pl.ANY),
    ]
    aliases = {}
    if into is not None:
        operands.append(into)
        in_specs.append(pl.BlockSpec(memory_space=pl.ANY))
        aliases = {4: 1}
    count = len(blocks)
    return pl.pallas_call(
        functools.partial(open_space_kernel, frame, blocks),
        out_shape=[
            jax.ShapeDtypeStruct((devices, count, per, features), jnp.bfloat16),
            jax.ShapeDtypeStruct((frames * sites, 3 * features), jnp.bfloat16),
        ],
        grid=(BLOCKS + count,),
        in_specs=in_specs,
        out_specs=[
            pl.BlockSpec(
                (devices, 1, per, features), lambda s: (0, jnp.maximum(s - BLOCKS, 0), 0, 0)
            ),
            pl.BlockSpec(memory_space=pl.ANY),
        ],
        scratch_shapes=[
            pltpu.VMEM((sites, 3 * features), jnp.bfloat16),
            pltpu.VMEM((block, features), jnp.float32),
            pltpu.VMEM(weights.shape, jnp.bfloat16),
            pltpu.SemaphoreType.DMA((BLOCKS + 1,)),
        ],
        input_output_aliases=aliases,
        compiler_params=pltpu.CompilerParams(vmem_limit_bytes=VMEM_LIMIT),
        cost_estimate=pl.CostEstimate(
            flops=2 * sites * features * 3 * features
            + 2 * count * block * (features * features + 2 * sites * HEADS * WINDOW),
            bytes_accessed=2 * features * (4 * sites + 2 * count * block + 4 * features),
            transcendentals=count * block * sites * HEADS,
        ),
        name="space_open",
    )(*operands)


def attend_space_kernel(x_ref, q_ref, k_ref, v_ref, mod_ref, w_ref, o_ref, total):
    attend_heads(
        lambda lane: q_ref[:, pl.ds(lane, WINDOW)],
        lambda lane: k_ref[:, pl.ds(lane, WINDOW)],
        lambda lane: v_ref[:, pl.ds(lane, WINDOW)],
        total,
        x_ref,
        mod_ref,
        w_ref,
        o_ref,
    )


def attend_space(video, triples, modulation, weights, group, devices):
    _, sites, features = video.shape
    block = sites // BLOCKS
    per = block // devices
    count = len(group)

    def frame(s):
        return pick(s, [f for f, _ in group])

    def place(s):
        return pick(s, [b for _, b in group])

    return pl.pallas_call(
        attend_space_kernel,
        out_shape=jax.ShapeDtypeStruct((devices, count, per, features), jnp.bfloat16),
        grid=(count,),
        in_specs=[
            pl.BlockSpec((1, block, features), lambda s: (frame(s), place(s), 0)),
            pl.BlockSpec((block, features), lambda s: (frame(s) * BLOCKS + place(s), 0)),
            pl.BlockSpec((sites, features), lambda s: (frame(s), 1)),
            pl.BlockSpec((sites, features), lambda s: (frame(s), 2)),
            pl.BlockSpec(modulation.shape, lambda s: (0, 0)),
            pl.BlockSpec(weights.shape, lambda s: (0, 0)),
        ],
        out_specs=pl.BlockSpec((devices, 1, per, features), lambda s: (0, s, 0, 0)),
        scratch_shapes=[pltpu.VMEM((block, features), jnp.float32)],
        compiler_params=pltpu.CompilerParams(vmem_limit_bytes=VMEM_LIMIT),
        cost_estimate=pl.CostEstimate(
            flops=2 * count * block * (features * features + 2 * sites * HEADS * WINDOW),
            bytes_accessed=2 * features * (3 * count * block + 2 * sites + features),
            transcendentals=count * block * sites * HEADS,
        ),
        name="space_attend",
    )(video, triples, triples, triples, modulation, weights)


def time_kernel(sources, mod_ref, wi_ref, wo_ref, *rest):
    o_ref, stream, triples, total = rest[-4:]
    step = pl.program_id(0)
    devices, frames, per, features = o_ref.shape
    groups = per // 8
    size = devices * frames * 8
    share = devices * 8
    for frame, refs in enumerate(sources):
        arrived = pick(step, [rest[index][:, 0] for index in refs]).astype(jnp.float32)
        for g in range(groups):
            stream[pl.ds(g * size + frame * share, share), :] = arrived[
                :, 8 * g : 8 * g + 8, :
            ].reshape(share, features)
    site_of_query = lax.broadcasted_iota(jnp.int32, (size, size), 0) % 8
    site_of_key = lax.broadcasted_iota(jnp.int32, (size, size), 1) % 8

    def one_group(g, carry):
        here = pl.ds(pl.multiple_of(g * size, size), size)
        half = size // 2

        def one_half(h, carry):
            start = pl.multiple_of(h * half, half)
            values = stream[pl.ds(pl.multiple_of(g * size + start, half), half), :]
            project(values, mod_ref, 3, wi_ref, triples, pl.ds(start, half))
            return carry

        lax.fori_loop(0, 2, one_half, 0)
        total[...] = jnp.zeros_like(total)

        def one_head(head, carry):
            scores = score_head(
                head,
                lambda lane: triples[:, pl.ds(lane, WINDOW)],
                lambda lane: triples[:, pl.ds(pl.multiple_of(features + lane, LANES), WINDOW)],
                size,
                features,
            )
            mix_head(
                head,
                jnp.where(site_of_query == site_of_key, scores, FAR),
                lambda lane: triples[:, pl.ds(pl.multiple_of(2 * features + lane, LANES), WINDOW)],
                total,
            )
            return carry

        lax.fori_loop(0, HEADS, one_head, 0, unroll=HEADS_AT_ONCE)
        branch = jnp.dot(
            total[...].astype(jnp.bfloat16), wo_ref[...], preferred_element_type=jnp.float32
        )
        stream[here, :] = stream[here, :] + mod_ref[5:6, :] * branch
        return carry

    lax.fori_loop(0, groups, one_group, 0)
    for frame in range(frames):
        o_ref[:, frame] = jnp.concatenate(
            [
                stream[pl.ds(g * size + frame * share, share), :].reshape(devices, 8, features)
                for g in range(groups)
            ],
            axis=1,
        ).astype(jnp.bfloat16)


def attend_time(arrived, blocks, frames, modulation, wide_weights, weights):
    operands = [modulation, wide_weights, weights]
    in_specs = [
        pl.BlockSpec(modulation.shape, lambda s: (0, 0)),
        pl.BlockSpec(wide_weights.shape, lambda s: (0, 0), pipeline_mode=pl.Buffered(1)),
        pl.BlockSpec(weights.shape, lambda s: (0, 0), pipeline_mode=pl.Buffered(1)),
    ]
    sources = []
    for frame in range(frames):
        arrays, slots, refs = [], [], []
        for block in blocks:
            array, slot = arrived[frame, block]
            known = [index for index, other in enumerate(arrays) if other is array]
            if not known:
                known = [len(arrays)]
                arrays.append(array)
                slots.append([])
            slots[known[0]].append(slot)
            refs.append(len(operands) - 3 + known[0])
        for array, places in zip(arrays, slots):
            devices, _, per, features = array.shape
            in_specs.append(
                pl.BlockSpec(
                    (devices, 1, per, features),
                    lambda s, places=places: (
                        0,
                        pick(s, places) if len(places) > 1 else places[0],
                        0,
                        0,
                    ),
                )
            )
            operands.append(array)
        sources.append(refs if len(arrays) > 1 else refs[:1])
    rows = devices * frames * per
    size = devices * frames * 8
    return pl.pallas_call(
        functools.partial(time_kernel, sources),
        out_shape=jax.ShapeDtypeStruct(
            (devices, frames, len(blocks) * per, features), jnp.bfloat16
        ),
        grid=(len(blocks),),
        in_specs=in_specs,
        out_specs=pl.BlockSpec((devices, frames, per, features), lambda s: (0, 0, s, 0)),
        scratch_shapes=[
            pltpu.VMEM((rows, features), jnp.float32),
            pltpu.VMEM((size, 3 * features), jnp.bfloat16),
            pltpu.VMEM((size, features), jnp.float32),
        ],
        compiler_params=pltpu.CompilerParams(vmem_limit_bytes=VMEM_LIMIT),
        cost_estimate=pl.CostEstimate(
            flops=len(blocks)
            * (
                2 * rows * features * 4 * features
                + 4 * rows * 8 * devices * frames * HEADS * WINDOW
            ),
            bytes_accessed=len(blocks) * 4 * rows * features + 8 * features * features,
            transcendentals=len(blocks) * rows * 8 * devices * frames * HEADS,
        ),
        name="time_block",
    )(*operands)


def place_sites(piece, into, first, count):
    owners, frames, sites, features = piece.shape
    per = sites // count

    def place_kernel(x_ref, *rest):
        o_hbm, semaphores = rest[-2:]
        copies = [
            pltpu.make_async_copy(
                x_ref.at[:, frame, pl.ds(block * per, per)],
                o_hbm.at[frame, pl.ds((first + block) * owners, owners)],
                semaphores.at[frame, block],
            )
            for frame in range(frames)
            for block in range(count)
        ]
        for copy in copies:
            copy.start()
        for copy in copies:
            copy.wait()

    operands = [piece]
    in_specs = [pl.BlockSpec(memory_space=pltpu.VMEM)]
    aliases = {}
    if into is not None:
        operands.append(into)
        in_specs.append(pl.BlockSpec(memory_space=pl.ANY))
        aliases = {1: 0}
    return pl.pallas_call(
        place_kernel,
        out_shape=jax.ShapeDtypeStruct((frames, BLOCKS * owners, per, features), jnp.bfloat16),
        in_specs=in_specs,
        out_specs=pl.BlockSpec(memory_space=pl.ANY),
        scratch_shapes=[pltpu.SemaphoreType.DMA((frames, count))],
        input_output_aliases=aliases,
        compiler_params=pltpu.CompilerParams(vmem_limit_bytes=PLACE_LIMIT),
        cost_estimate=pl.CostEstimate(
            flops=0, bytes_accessed=4 * piece.size, transcendentals=0
        ),
        name="place_sites",
    )(*operands)


def exchange(pieces, earlier):
    if earlier is not None:
        pieces, earlier = lax.optimization_barrier((pieces, earlier))
    return lax.all_to_all(pieces, "wide", split_axis=0, concat_axis=0, tiled=True), earlier


def on_device(video, modulation, spatial_input, spatial_output, temporal_input, temporal_output):
    frames, sites, features = video.shape
    devices = lax.axis_size("wide")
    triples = None
    opened = set()
    landings = []
    arrived = {}
    landed = None
    for group in departures(frames):
        fresh = sorted({frame for frame, _ in group} - opened)
        if len(fresh) == 1 and {frame for frame, _ in group} == set(fresh):
            leaving, triples = open_space(
                video,
                modulation,
                spatial_input,
                spatial_output,
                fresh[0],
                [block for _, block in group],
                triples,
                devices,
            )
            opened.update(fresh)
        else:
            leaving = attend_space(video, triples, modulation, spatial_output, group, devices)
        leaving, triples = lax.optimization_barrier((leaving, triples))
        landed, earlier = exchange(leaving, landed)
        landings[-1:] = [earlier, landed] if landings else [landed]
        for slot, pair in enumerate(group):
            arrived[pair] = len(landings) - 1, slot
    refined = None
    for blocks in RETURNS:
        done = attend_time(
            {pair: (landings[index], slot) for pair, (index, slot) in arrived.items()},
            blocks,
            frames,
            modulation,
            temporal_input,
            temporal_output,
        )
        last = landed is landings[-1]
        landed, earlier = exchange(done, landed)
        if last:
            landings[-1] = earlier
        else:
            back = earlier
            refined = place_sites(back, refined, previous[0], len(previous))
        previous = blocks
    refined = place_sites(landed, refined, previous[0], len(previous))
    return refined.reshape(video.shape)


def solution(mesh):
    placed = (P(("groups", "wide"), None, None), P("groups", None), P(), P(), P(), P())
    return jax.shard_map(
        on_device,
        mesh=mesh,
        in_specs=placed,
        out_specs=P(("groups", "wide"), None, None),
        check_vma=False,
    )
```

```python
import functools
import math

import jax
import jax.numpy as jnp
from jax import lax
from jax.experimental import pallas as pl
from jax.experimental.pallas import tpu as pltpu
from jax.sharding import PartitionSpec as P

HEADS = 16
HEAD_DIM = 72
EPSILON = 1e-06
SCORE_SCALE = math.log2(math.e) / math.sqrt(HEAD_DIM)
LANES = 128
WINDOW = 2 * LANES
FAR = -1e30
VMEM_LIMIT = 63 * 1024 * 1024
PLACE_LIMIT = 16 * 1024 * 1024
BLOCKS = 4
RETURNS = ((0, 1), (2, 3))
HEADS_AT_ONCE = 4


def departures(frames):
    if frames == 2:
        return (((0, 0), (0, 1)), ((1, 0), (1, 1)), ((0, 2), (0, 3), (1, 2), (1, 3)))
    whole = [tuple((frame, block) for frame in range(frames)) for block in range(BLOCKS)]
    return (whole[0], whole[1], whole[2] + whole[3])


def pick(step, values):
    chosen = values[0]
    for index in range(1, len(values)):
        chosen = jnp.where(step == index, values[index], chosen)
    return chosen


def normalize(values, offset_row, stretch):
    average = jnp.mean(values, axis=-1, keepdims=True)
    centered = values - average
    spread = jnp.mean(centered * centered, axis=-1, keepdims=True)
    return (centered * lax.rsqrt(spread + EPSILON) * (1.0 + stretch) + offset_row).astype(
        jnp.bfloat16
    )


def head_window(head, features):
    last = features // LANES - 2
    if isinstance(head, int):
        tile = min(head * HEAD_DIM // LANES, last)
        return tile * LANES, head * HEAD_DIM - tile * LANES
    tile = jnp.minimum(head * HEAD_DIM // LANES, last)
    return pl.multiple_of(tile * LANES, LANES), head * HEAD_DIM - tile * LANES


def in_head(rows, first):
    lanes = lax.broadcasted_iota(jnp.int32, (rows, WINDOW), 1)
    return (lanes >= first) & (lanes < first + HEAD_DIM)


def score_head(head, q_of, k_of, rows, features):
    lane, first = head_window(head, features)
    return lax.dot_general(
        jnp.where(in_head(rows, first), q_of(lane), 0),
        k_of(lane),
        (((1,), (1,)), ((), ())),
        preferred_element_type=jnp.float32,
    )


def mix_head(head, scores, v_of, total):
    rows, features = total.shape
    lane, first = head_window(head, features)
    largest = jnp.max(scores, axis=-1, keepdims=True)
    powers = jnp.exp2(scores - largest)
    weight = jnp.sum(powers, axis=-1, keepdims=True)
    mixed = jnp.dot(powers.astype(jnp.bfloat16), v_of(lane), preferred_element_type=jnp.float32)
    mixed = jnp.where(in_head(rows, first), mixed * (1.0 / weight), 0.0)
    total[:, pl.ds(lane, WINDOW)] = total[:, pl.ds(lane, WINDOW)] + mixed


def attend_heads(q_of, k_of, v_of, total, x_ref, mod_ref, w_ref, o_ref):
    rows, features = total.shape
    total[...] = jnp.zeros_like(total)
    scores = score_head(0, q_of, k_of, rows, features)
    for head in range(HEADS):
        following = None
        if head + 1 < HEADS:
            following = score_head(head + 1, q_of, k_of, rows, features)
        mix_head(head, scores, v_of, total)
        scores = following
    branch = jnp.dot(
        total[...].astype(jnp.bfloat16), w_ref[...], preferred_element_type=jnp.float32
    )
    halfway = x_ref[0].astype(jnp.float32) + mod_ref[2:3, :] * branch
    o_ref[...] = halfway.astype(jnp.bfloat16).reshape(o_ref.shape)


def project(values, mod_ref, row, w_ref, target, rows):
    features = values.shape[1]
    normed = normalize(values, mod_ref[row : row + 1, :], mod_ref[row + 1 : row + 2, :])
    product = jnp.dot(normed, w_ref[...], preferred_element_type=jnp.float32)
    target[rows, :features] = (product[:, :features] * SCORE_SCALE).astype(jnp.bfloat16)
    target[rows, features:] = product[:, features:].astype(jnp.bfloat16)


def open_space_kernel(frame, blocks, x_ref, mod_ref, wi_ref, wo_hbm, *rest):
    o_ref, t_hbm, triples, total, wo_ref, semaphores = rest[-6:]
    step = pl.program_id(0)
    _, rows, features = x_ref.shape
    sites = triples.shape[0]
    count = sites // rows

    def keep(block):
        here = pl.ds(pl.multiple_of(block * rows, rows), rows)
        there = pl.ds(pl.multiple_of(frame * sites + block * rows, rows), rows)
        return pltpu.make_async_copy(triples.at[here], t_hbm.at[there], semaphores.at[block])

    fetch = pltpu.make_async_copy(wo_hbm, wo_ref, semaphores.at[count])
    pl.when(step == 0)(fetch.start)
    pl.when(step == count)(fetch.wait)

    @pl.when(step < count)
    def _():
        here = pl.ds(pl.multiple_of(step * rows, rows), rows)
        project(x_ref[0].astype(jnp.float32), mod_ref, 0, wi_ref, triples, here)
        keep(step).start()

    @pl.when(step >= count)
    def _():
        first = pl.multiple_of(pick(step - count, blocks) * rows, rows)
        attend_heads(
            lambda lane: triples[pl.ds(first, rows), pl.ds(lane, WINDOW)],
            lambda lane: triples[:, pl.ds(features + lane, WINDOW)],
            lambda lane: triples[:, pl.ds(2 * features + lane, WINDOW)],
            total,
            x_ref,
            mod_ref,
            wo_ref,
            o_ref,
        )

    @pl.when(step == count + len(blocks) - 1)
    def _():
        for block in range(count):
            keep(block).wait()


def open_space(video, modulation, wide_weights, weights, frame, blocks, into, devices):
    frames, sites, features = video.shape
    block = sites // BLOCKS
    per = block // devices
    operands = [video, modulation, wide_weights, weights]
    in_specs = [
        pl.BlockSpec(
            (1, block, features),
            lambda s: (frame, jnp.where(s < BLOCKS, s, pick(s - BLOCKS, blocks)), 0),
        ),
        pl.BlockSpec(modulation.shape, lambda s: (0, 0)),
        pl.BlockSpec(wide_weights.shape, lambda s: (0, 0), pipeline_mode=pl.Buffered(1)),
        pl.BlockSpec(memory_space=pl.ANY),
    ]
    aliases = {}
    if into is not None:
        operands.append(into)
        in_specs.append(pl.BlockSpec(memory_space=pl.ANY))
        aliases = {4: 1}
    count = len(blocks)
    return pl.pallas_call(
        functools.partial(open_space_kernel, frame, blocks),
        out_shape=[
            jax.ShapeDtypeStruct((devices, count, per, features), jnp.bfloat16),
            jax.ShapeDtypeStruct((frames * sites, 3 * features), jnp.bfloat16),
        ],
        grid=(BLOCKS + count,),
        in_specs=in_specs,
        out_specs=[
            pl.BlockSpec(
                (devices, 1, per, features), lambda s: (0, jnp.maximum(s - BLOCKS, 0), 0, 0)
            ),
            pl.BlockSpec(memory_space=pl.ANY),
        ],
        scratch_shapes=[
            pltpu.VMEM((sites, 3 * features), jnp.bfloat16),
            pltpu.VMEM((block, features), jnp.float32),
            pltpu.VMEM(weights.shape, jnp.bfloat16),
            pltpu.SemaphoreType.DMA((BLOCKS + 1,)),
        ],
        input_output_aliases=aliases,
        compiler_params=pltpu.CompilerParams(vmem_limit_bytes=VMEM_LIMIT),
        cost_estimate=pl.CostEstimate(
            flops=2 * sites * features * 3 * features
            + 2 * count * block * (features * features + 2 * sites * HEADS * WINDOW),
            bytes_accessed=2 * features * (4 * sites + 2 * count * block + 4 * features),
            transcendentals=count * block * sites * HEADS,
        ),
        name="space_open",
    )(*operands)


def attend_space_kernel(x_ref, q_ref, k_ref, v_ref, mod_ref, w_ref, o_ref, total):
    attend_heads(
        lambda lane: q_ref[:, pl.ds(lane, WINDOW)],
        lambda lane: k_ref[:, pl.ds(lane, WINDOW)],
        lambda lane: v_ref[:, pl.ds(lane, WINDOW)],
        total,
        x_ref,
        mod_ref,
        w_ref,
        o_ref,
    )


def attend_space(video, triples, modulation, weights, group, devices):
    _, sites, features = video.shape
    block = sites // BLOCKS
    per = block // devices
    count = len(group)

    def frame(s):
        return pick(s, [f for f, _ in group])

    def place(s):
        return pick(s, [b for _, b in group])

    return pl.pallas_call(
        attend_space_kernel,
        out_shape=jax.ShapeDtypeStruct((devices, count, per, features), jnp.bfloat16),
        grid=(count,),
        in_specs=[
            pl.BlockSpec((1, block, features), lambda s: (frame(s), place(s), 0)),
            pl.BlockSpec((block, features), lambda s: (frame(s) * BLOCKS + place(s), 0)),
            pl.BlockSpec((sites, features), lambda s: (frame(s), 1)),
            pl.BlockSpec((sites, features), lambda s: (frame(s), 2)),
            pl.BlockSpec(modulation.shape, lambda s: (0, 0)),
            pl.BlockSpec(weights.shape, lambda s: (0, 0)),
        ],
        out_specs=pl.BlockSpec((devices, 1, per, features), lambda s: (0, s, 0, 0)),
        scratch_shapes=[pltpu.VMEM((block, features), jnp.float32)],
        compiler_params=pltpu.CompilerParams(vmem_limit_bytes=VMEM_LIMIT),
        cost_estimate=pl.CostEstimate(
            flops=2 * count * block * (features * features + 2 * sites * HEADS * WINDOW),
            bytes_accessed=2 * features * (3 * count * block + 2 * sites + features),
            transcendentals=count * block * sites * HEADS,
        ),
        name="space_attend",
    )(video, triples, triples, triples, modulation, weights)


def time_kernel(sources, mod_ref, wi_ref, wo_ref, *rest):
    o_ref, stream, triples, total = rest[-4:]
    step = pl.program_id(0)
    devices, frames, per, features = o_ref.shape
    groups = per // 8
    size = devices * frames * 8
    share = devices * 8
    for frame, refs in enumerate(sources):
        arrived = pick(step, [rest[index][:, 0] for index in refs]).astype(jnp.float32)
        for g in range(groups):
            stream[pl.ds(g * size + frame * share, share), :] = arrived[
                :, 8 * g : 8 * g + 8, :
            ].reshape(share, features)
    site_of_query = lax.broadcasted_iota(jnp.int32, (size, size), 0) % 8
    site_of_key = lax.broadcasted_iota(jnp.int32, (size, size), 1) % 8

    def one_group(g, carry):
        here = pl.ds(pl.multiple_of(g * size, size), size)
        half = size // 2

        def one_half(h, carry):
            start = pl.multiple_of(h * half, half)
            values = stream[pl.ds(pl.multiple_of(g * size + start, half), half), :]
            project(values, mod_ref, 3, wi_ref, triples, pl.ds(start, half))
            return carry

        lax.fori_loop(0, 2, one_half, 0)
        total[...] = jnp.zeros_like(total)

        def one_head(head, carry):
            scores = score_head(
                head,
                lambda lane: triples[:, pl.ds(lane, WINDOW)],
                lambda lane: triples[:, pl.ds(pl.multiple_of(features + lane, LANES), WINDOW)],
                size,
                features,
            )
            mix_head(
                head,
                jnp.where(site_of_query == site_of_key, scores, FAR),
                lambda lane: triples[:, pl.ds(pl.multiple_of(2 * features + lane, LANES), WINDOW)],
                total,
            )
            return carry

        lax.fori_loop(0, HEADS, one_head, 0, unroll=HEADS_AT_ONCE)
        branch = jnp.dot(
            total[...].astype(jnp.bfloat16), wo_ref[...], preferred_element_type=jnp.float32
        )
        stream[here, :] = stream[here, :] + mod_ref[5:6, :] * branch
        return carry

    lax.fori_loop(0, groups, one_group, 0)
    for frame in range(frames):
        o_ref[:, frame] = jnp.concatenate(
            [
                stream[pl.ds(g * size + frame * share, share), :].reshape(devices, 8, features)
                for g in range(groups)
            ],
            axis=1,
        ).astype(jnp.bfloat16)


def attend_time(arrived, blocks, frames, modulation, wide_weights, weights):
    operands = [modulation, wide_weights, weights]
    in_specs = [
        pl.BlockSpec(modulation.shape, lambda s: (0, 0)),
        pl.BlockSpec(wide_weights.shape, lambda s: (0, 0), pipeline_mode=pl.Buffered(1)),
        pl.BlockSpec(weights.shape, lambda s: (0, 0), pipeline_mode=pl.Buffered(1)),
    ]
    sources = []
    for frame in range(frames):
        arrays, slots, refs = [], [], []
        for block in blocks:
            array, slot = arrived[frame, block]
            known = [index for index, other in enumerate(arrays) if other is array]
            if not known:
                known = [len(arrays)]
                arrays.append(array)
                slots.append([])
            slots[known[0]].append(slot)
            refs.append(len(operands) - 3 + known[0])
        for array, places in zip(arrays, slots):
            devices, _, per, features = array.shape
            in_specs.append(
                pl.BlockSpec(
                    (devices, 1, per, features),
                    lambda s, places=places: (
                        0,
                        pick(s, places) if len(places) > 1 else places[0],
                        0,
                        0,
                    ),
                )
            )
            operands.append(array)
        sources.append(refs if len(arrays) > 1 else refs[:1])
    rows = devices * frames * per
    size = devices * frames * 8
    return pl.pallas_call(
        functools.partial(time_kernel, sources),
        out_shape=jax.ShapeDtypeStruct(
            (devices, frames, len(blocks) * per, features), jnp.bfloat16
        ),
        grid=(len(blocks),),
        in_specs=in_specs,
        out_specs=pl.BlockSpec((devices, frames, per, features), lambda s: (0, 0, s, 0)),
        scratch_shapes=[
            pltpu.VMEM((rows, features), jnp.float32),
            pltpu.VMEM((size, 3 * features), jnp.bfloat16),
            pltpu.VMEM((size, features), jnp.float32),
        ],
        compiler_params=pltpu.CompilerParams(vmem_limit_bytes=VMEM_LIMIT),
        cost_estimate=pl.CostEstimate(
            flops=len(blocks)
            * (
                2 * rows * features * 4 * features
                + 4 * rows * 8 * devices * frames * HEADS * WINDOW
            ),
            bytes_accessed=len(blocks) * 4 * rows * features + 8 * features * features,
            transcendentals=len(blocks) * rows * 8 * devices * frames * HEADS,
        ),
        name="time_block",
    )(*operands)


def place_sites(piece, into, first, count):
    owners, frames, sites, features = piece.shape
    per = sites // count

    def place_kernel(x_ref, *rest):
        o_hbm, semaphores = rest[-2:]
        copies = [
            pltpu.make_async_copy(
                x_ref.at[:, frame, pl.ds(block * per, per)],
                o_hbm.at[frame, pl.ds((first + block) * owners, owners)],
                semaphores.at[frame, block],
            )
            for frame in range(frames)
            for block in range(count)
        ]
        for copy in copies:
            copy.start()
        for copy in copies:
            copy.wait()

    operands = [piece]
    in_specs = [pl.BlockSpec(memory_space=pltpu.VMEM)]
    aliases = {}
    if into is not None:
        operands.append(into)
        in_specs.append(pl.BlockSpec(memory_space=pl.ANY))
        aliases = {1: 0}
    return pl.pallas_call(
        place_kernel,
        out_shape=jax.ShapeDtypeStruct((frames, BLOCKS * owners, per, features), jnp.bfloat16),
        in_specs=in_specs,
        out_specs=pl.BlockSpec(memory_space=pl.ANY),
        scratch_shapes=[pltpu.SemaphoreType.DMA((frames, count))],
        input_output_aliases=aliases,
        compiler_params=pltpu.CompilerParams(vmem_limit_bytes=PLACE_LIMIT),
        cost_estimate=pl.CostEstimate(
            flops=0, bytes_accessed=4 * piece.size, transcendentals=0
        ),
        name="place_sites",
    )(*operands)


def exchange(pieces, earlier):
    if earlier is not None:
        pieces, earlier = lax.optimization_barrier((pieces, earlier))
    flat = pieces.reshape(pieces.shape[0], -1, pieces.shape[-1])
    landed = lax.all_to_all(flat, "wide", split_axis=0, concat_axis=0, tiled=True)
    return landed.reshape(pieces.shape), earlier


def on_device(video, modulation, spatial_input, spatial_output, temporal_input, temporal_output):
    frames, sites, features = video.shape
    devices = lax.axis_size("wide")
    triples = None
    opened = set()
    landings = []
    arrived = {}
    landed = None
    for group in departures(frames):
        fresh = sorted({frame for frame, _ in group} - opened)
        if len(fresh) == 1 and {frame for frame, _ in group} == set(fresh):
            leaving, triples = open_space(
                video,
                modulation,
                spatial_input,
                spatial_output,
                fresh[0],
                [block for _, block in group],
                triples,
                devices,
            )
            opened.update(fresh)
        else:
            leaving = attend_space(video, triples, modulation, spatial_output, group, devices)
        leaving, triples = lax.optimization_barrier((leaving, triples))
        landed, earlier = exchange(leaving, landed)
        landings[-1:] = [earlier, landed] if landings else [landed]
        for slot, pair in enumerate(group):
            arrived[pair] = len(landings) - 1, slot
    refined = None
    for blocks in RETURNS:
        done = attend_time(
            {pair: (landings[index], slot) for pair, (index, slot) in arrived.items()},
            blocks,
            frames,
            modulation,
            temporal_input,
            temporal_output,
        )
        last = landed is landings[-1]
        landed, earlier = exchange(done, landed)
        if last:
            landings[-1] = earlier
        else:
            back = earlier
            refined = place_sites(back, refined, previous[0], len(previous))
        previous = blocks
    refined = place_sites(landed, refined, previous[0], len(previous))
    return refined.reshape(video.shape)


def solution(mesh):
    placed = (P(("groups", "wide"), None, None), P("groups", None), P(), P(), P(), P())
    return jax.shard_map(
        on_device,
        mesh=mesh,
        in_specs=placed,
        out_specs=P(("groups", "wide"), None, None),
        check_vma=False,
    )
```
